1024 devices in a mesh: grp: 32 (over y_lo, z), inner: 32 (over y_hi, x, core).
Axes of the slice: x: 8, y: 8 (y_hi: 2, y_lo: 4; y = y_hi * 4 + y_lo), z: 8, core: 2. Of those that a mesh axis runs over, the one named last changes fastest.
Arguments:
- b_tensor: bfloat16 [10, 8192, 3072], P(None, ('grp', 'inner')), may hold values from -0.59765625 to 0.59765625
- occ_energy: float32 [10], replicated, may hold values from -2 to -0.5
- vir_energy: float32 [3072], replicated, may hold values from 0.5 to 4
- left_list: int32 [3], replicated, may hold values from 0 to 9
- right_occ: int32 [1], replicated, may hold values from 0 to 9
Outputs:
- gamma_aux: float32 [10, 8192, 3072], P(None, ('grp', 'inner'))
The draws below stay inside these ranges and needn't reach their ends.
Inputs may be any that keep to these rules, and one draw needn't show every extreme that they name: `left_list`: each entry is an occupied orbital of the window; a first orbital may equal the second, and first orbitals may repeat. `right_occ`: an occupied orbital of the window.
All inputs are finite; a program needn't handle non-finite values.
Results may differ from the reference program's by a relative error of at most 0.0023.
Values may be sent and summed in bfloat16 or wider, within the bound.
No kernel may reach another device: no remote copies, remote signals or barrier semaphores. Data moves between devices by JAX's collectives and lax.ppermute only.
A program may use at most 32 MiB of HBM per device.

```python
import jax
import jax.numpy as jnp
from jax import lax

OCC_W = 10
NI = 3
V = 3072
AUX = 8192
N_GRP = 32


def level_of(rng, dims, pieces, low, top_value):
    gain = 1.0
    for dim, parts in pieces:
        draws = jax.random.uniform(jax.random.fold_in(jax.random.fold_in(rng, 6), dim), (parts,), jnp.float32, low / len(pieces), top_value / len(pieces))
        gain = gain * jnp.repeat(jnp.exp(draws), dims[dim] // parts).reshape((-1,) + (1,) * (len(dims) - 1 - dim))
    return gain


def scatter_about(rng, shape, spread, most, cuts=(), dtype=jnp.bfloat16):
    entries = jax.random.normal(rng, shape, jnp.float32) * spread
    if len(cuts) > 0:
        entries = level_of(rng, shape, cuts, -0.22, 0.18) * entries
    return jnp.clip(entries, min=-most, max=most).astype(dtype)


def setup_inputs(seed: int = 0) -> dict:
    seeds = jax.random.split(jax.random.key(seed), 6)
    return {
        "b_tensor": scatter_about(seeds[0], (OCC_W, AUX, V), 0.1, 0.59765625, ((1, 1024),)),
        "occ_energy": jnp.clip(jax.random.uniform(seeds[1], (OCC_W,), jnp.float32, -2.0, -0.5), -2.0, -0.5),
        "vir_energy": jnp.clip(jax.random.uniform(seeds[2], (V,), jnp.float32, 0.5, 4.0), 0.5, 4.0),
        "left_list": jax.random.randint(seeds[3], (NI,), 0, OCC_W).astype(jnp.int32),
        "right_occ": jax.random.randint(seeds[4], (1,), 0, OCC_W).astype(jnp.int32),
    }


def add_group(total, blocks):
    left, right = blocks
    partial_value = lax.dot_general(left, right, (((0,), (0,)), ((), ())), preferred_element_type=jnp.float32)
    return total + partial_value, None


def reference(b_tensor, occ_energy, vir_energy, left_list, right_occ):
    gamma_aux = jnp.zeros((OCC_W, AUX, V), jnp.float32)
    second_occ = right_occ[0].astype(jnp.int32)
    block_right = lax.dynamic_index_in_dim(b_tensor, second_occ, 0, keepdims=False)
    grouped_right = block_right.reshape(N_GRP, AUX // N_GRP, V)
    for pair_no in range(NI):
        left_occ = left_list[pair_no].astype(jnp.int32)
        block_left = lax.dynamic_index_in_dim(b_tensor, left_occ, 0, keepdims=False)
        grouped_left = block_left.reshape(N_GRP, AUX // N_GRP, V)
        integral, unused = lax.scan(add_group, jnp.zeros((V, V), jnp.float32), (grouped_left, grouped_right))
        shift_occ = occ_energy[left_occ] + occ_energy[second_occ]
        denominator = shift_occ - vir_energy[:, None] - vir_energy[None, :]
        amplitude = (integral / denominator).astype(jnp.bfloat16)
        contribution = lax.dot_general(block_right, amplitude, (((1,), (1,)), ((), ())), preferred_element_type=jnp.float32)
        gamma_aux = gamma_aux.at[left_occ].add(contribution)
    return gamma_aux
```

```python
import jax
import jax.numpy as jnp
import numpy as np
from jax import lax
from jax.sharding import Mesh, PartitionSpec as P

GRP_BITS = ("y1", "y0", "z2", "z1", "z0")
INNER_BITS = ("y2", "x2", "x1", "x0", "c")
ALL_BITS = GRP_BITS + INNER_BITS
A_BITS = ("x2", "x1", "y2", "y1")
B_BITS = ("z2", "z1")
AB_BITS = A_BITS + B_BITS
B_SUM_BITS = ("c",)
A_SUM_BITS = ("x0", "y0", "z0")
SUM_BITS = B_SUM_BITS + A_SUM_BITS


def exchange(x, axes):
    return lax.all_to_all(x, axes, split_axis=0, concat_axis=0, tiled=True)


def body(b_tensor, occ_energy, vir_energy, left_list, right_occ):
    occ_count, rows, virtuals = b_tensor.shape
    pairs = left_list.shape[0]
    a_parts, b_parts = 2 ** len(A_BITS), 2 ** len(B_BITS)
    a_subs, b_subs = 2 ** len(A_SUM_BITS), 2 ** len(B_SUM_BITS)
    a_width, b_width = virtuals // a_parts, virtuals // b_parts
    pa_width = pairs * a_width
    sub_rows, sub_cols = pa_width // a_subs, b_width // b_subs
    peers, subs = a_parts * b_parts, a_subs * b_subs
    group_rows = peers * rows

    second_occ = right_occ[0]
    block_right = lax.dynamic_index_in_dim(b_tensor, second_occ, 0, keepdims=False)
    block_left = jnp.stack(
        [lax.dynamic_index_in_dim(b_tensor, left_list[p], 0, keepdims=False) for p in range(pairs)]
    )

    to_b = block_right.reshape(rows, b_parts, b_width).transpose(1, 0, 2)
    to_a = block_left.reshape(pairs, rows, a_parts, a_width).transpose(2, 1, 0, 3).reshape(a_parts, rows, pa_width)
    packed = jnp.concatenate(
        [
            jnp.broadcast_to(to_b[None], (a_parts, b_parts, rows, b_width)),
            jnp.broadcast_to(to_a[:, None], (a_parts, b_parts, rows, pa_width)),
        ],
        axis=-1,
    )
    got = exchange(packed.reshape(peers, rows, b_width + pa_width), AB_BITS)
    got = got.reshape(group_rows, b_width + pa_width)
    right = got[:, :b_width].reshape(group_rows, b_subs, sub_cols)
    left = got[:, b_width:]

    partial_value = lax.dot_general(left, right, (((0,), (0,)), ((), ())), preferred_element_type=jnp.float32)
    partial_value = partial_value.transpose(1, 0, 2).reshape(subs, sub_rows, sub_cols)
    shares = exchange(partial_value, SUM_BITS).sum(axis=0)

    a_rank, b_rank = lax.axis_index(A_BITS), lax.axis_index(B_BITS)
    a_sub, b_sub = lax.axis_index(A_SUM_BITS), lax.axis_index(B_SUM_BITS)
    vir_a = lax.dynamic_slice_in_dim(vir_energy, a_rank * a_width, a_width)
    shift = occ_energy[left_list] + occ_energy[second_occ]
    row_part = (shift[:, None] - vir_a[None, :]).reshape(pa_width)
    row_part = lax.dynamic_slice_in_dim(row_part, a_sub * sub_rows, sub_rows)
    vir_b = lax.dynamic_slice_in_dim(vir_energy, b_rank * b_width + b_sub * sub_cols, sub_cols)
    denominator = row_part[:, None] - vir_b[None, :]
    amp_tile = (shares / denominator).astype(jnp.bfloat16)

    amps = exchange(jnp.broadcast_to(amp_tile[None], (subs, sub_rows, sub_cols)), SUM_BITS)
    amps = amps.reshape(b_subs, pa_width, sub_cols)
    contrib = lax.dot_general(right, amps, (((1, 2), (0, 2)), ((), ())), preferred_element_type=jnp.float32)
    returned = exchange(contrib.reshape(peers, rows, pa_width), AB_BITS)
    returned = returned.reshape(a_parts, b_parts, rows, pairs, a_width).sum(axis=1)
    returned = returned.transpose(2, 1, 0, 3).reshape(pairs, rows, virtuals)

    orbitals = jnp.arange(occ_count, dtype=jnp.int32)
    gamma_aux = jnp.zeros(b_tensor.shape, jnp.float32)
    for p in range(pairs):
        chosen = (orbitals == left_list[p]).astype(jnp.float32)
        gamma_aux = gamma_aux + chosen[:, None, None] * returned[p][None]
    return gamma_aux


def solution(mesh):
    fine = Mesh(np.asarray(mesh.devices).reshape((2,) * len(ALL_BITS)), ALL_BITS)
    placed = (P(None, ALL_BITS, None), P(), P(), P(), P())
    return jax.shard_map(body, mesh=fine, in_specs=placed, out_specs=P(None, ALL_BITS, None), check_vma=False)
```

```python
import jax
import jax.numpy as jnp
import numpy as np
from jax import lax
from jax.experimental import pallas as pl
from jax.experimental.pallas import tpu as pltpu
from jax.sharding import Mesh, PartitionSpec as P

GRP_BITS = ("y1", "y0", "z2", "z1", "z0")
INNER_BITS = ("y2", "x2", "x1", "x0", "c")
ALL_BITS = GRP_BITS + INNER_BITS
A_BITS = ("x2", "x1", "y2", "y1")
B_BITS = ("z2", "z1")
AB_BITS = A_BITS + B_BITS
B_SUM_BITS = ("c",)
A_SUM_BITS = ("x0", "y0", "z0")
SUM_BITS = B_SUM_BITS + A_SUM_BITS
INTERPRET = False


def exchange(x, axes):
    return lax.all_to_all(x, axes, split_axis=0, concat_axis=0, tiled=True)


def pack_rows(left_list, right_occ, b_tensor, a_parts, b_parts):
    _, rows, virtuals = b_tensor.shape
    pairs = left_list.shape[0]
    a_width, b_width = virtuals // a_parts, virtuals // b_parts

    def kernel(left_ref, right_ref, b_ref, out_ref, buf, sems):
        copies = []
        for p in range(pairs + 1):
            orbital = right_ref[0] if p == pairs else left_ref[p]
            copies.append(pltpu.make_async_copy(b_ref.at[orbital], buf.at[p], sems.at[p]))
            copies[-1].start()
        for p in range(pairs):
            copies[p].wait()
            start = b_width + p * a_width
            for a in range(a_parts):
                piece = buf[p, :, a * a_width : (a + 1) * a_width]
                for b in range(b_parts):
                    out_ref[a * b_parts + b, :, start : start + a_width] = piece
        copies[pairs].wait()
        for b in range(b_parts):
            piece = buf[pairs, :, b * b_width : (b + 1) * b_width]
            for a in range(a_parts):
                out_ref[a * b_parts + b, :, :b_width] = piece

    return pl.pallas_call(
        kernel,
        out_shape=jax.ShapeDtypeStruct((a_parts * b_parts, rows, b_width + pairs * a_width), b_tensor.dtype),
        in_specs=[
            pl.BlockSpec(memory_space=pltpu.SMEM),
            pl.BlockSpec(memory_space=pltpu.SMEM),
            pl.BlockSpec(memory_space=pl.ANY),
        ],
        out_specs=pl.BlockSpec(memory_space=pltpu.VMEM),
        scratch_shapes=[pltpu.VMEM((pairs + 1, rows, virtuals), b_tensor.dtype), pltpu.SemaphoreType.DMA((pairs + 1,))],
        interpret=INTERPRET,
    )(left_list, right_occ, b_tensor)


def place_rows(left_list, returned, occ_count, a_parts, b_parts):
    _, rows, pa_width = returned.shape
    pairs = left_list.shape[0]
    a_width = pa_width // pairs
    virtuals = a_parts * a_width

    def kernel(left_ref, in_ref, out_ref, rows_ref):
        for a in range(a_parts):
            total = in_ref[a * b_parts].astype(jnp.float32)
            for b in range(1, b_parts):
                total = total + in_ref[a * b_parts + b].astype(jnp.float32)
            for p in range(pairs):
                rows_ref[p, :, a * a_width : (a + 1) * a_width] = total[:, p * a_width : (p + 1) * a_width]
        for orbital in range(occ_count):
            total = jnp.zeros((rows, virtuals), jnp.float32)
            for p in range(pairs):
                total = total + jnp.where(left_ref[p] == orbital, rows_ref[p], 0.0)
            out_ref[orbital] = total

    return pl.pallas_call(
        kernel,
        out_shape=jax.ShapeDtypeStruct((occ_count, rows, virtuals), jnp.float32),
        in_specs=[pl.BlockSpec(memory_space=pltpu.SMEM), pl.BlockSpec(memory_space=pltpu.VMEM)],
        out_specs=pl.BlockSpec(memory_space=pltpu.VMEM),
        scratch_shapes=[pltpu.VMEM((pairs, rows, virtuals), jnp.float32)],
        interpret=INTERPRET,
    )(left_list, returned)


def body(b_tensor, occ_energy, vir_energy, left_list, right_occ):
    occ_count, rows, virtuals = b_tensor.shape
    pairs = left_list.shape[0]
    a_parts, b_parts = 2 ** len(A_BITS), 2 ** len(B_BITS)
    a_subs, b_subs = 2 ** len(A_SUM_BITS), 2 ** len(B_SUM_BITS)
    a_width, b_width = virtuals // a_parts, virtuals // b_parts
    pa_width = pairs * a_width
    sub_rows, sub_cols = pa_width // a_subs, b_width // b_subs
    peers, subs = a_parts * b_parts, a_subs * b_subs
    group_rows = peers * rows

    second_occ = right_occ[0]
    packed = pack_rows(left_list, right_occ, b_tensor, a_parts, b_parts)
    got = exchange(packed, AB_BITS)
    got = got.reshape(group_rows, b_width + pa_width)
    right = got[:, :b_width]
    left = got[:, b_width:]

    b_sub = lax.axis_index(B_SUM_BITS)

    def partial_of(half):
        cols = lax.dynamic_slice_in_dim(right, half * sub_cols, sub_cols, axis=1)
        return lax.dot_general(left, cols, (((0,), (0,)), ((), ())), preferred_element_type=jnp.float32)

    received = lax.ppermute(partial_of(1 - b_sub), B_SUM_BITS, [(0, 1), (1, 0)])
    own = lax.optimization_barrier(partial_of(b_sub))
    paired = own + received
    shares = exchange(paired.reshape(a_subs, sub_rows, sub_cols), A_SUM_BITS).sum(axis=0)

    a_rank, b_rank = lax.axis_index(A_BITS), lax.axis_index(B_BITS)
    a_sub = lax.axis_index(A_SUM_BITS)
    vir_a = lax.dynamic_slice_in_dim(vir_energy, a_rank * a_width, a_width)
    shift = occ_energy[left_list] + occ_energy[second_occ]
    row_part = (shift[:, None] - vir_a[None, :]).reshape(pa_width)
    row_part = lax.dynamic_slice_in_dim(row_part, a_sub * sub_rows, sub_rows)
    vir_b = lax.dynamic_slice_in_dim(vir_energy, b_rank * b_width + b_sub * sub_cols, sub_cols)
    denominator = row_part[:, None] - vir_b[None, :]
    amp_tile = (shares / denominator).astype(jnp.bfloat16)

    amps = exchange(jnp.broadcast_to(amp_tile[None], (subs, sub_rows, sub_cols)), SUM_BITS)
    amps = amps.reshape(b_subs, pa_width, sub_cols)
    halves = right.reshape(group_rows, b_subs, sub_cols)
    contrib = lax.dot_general(halves, amps, (((1, 2), (0, 2)), ((), ())), preferred_element_type=jnp.float32)
    returned = exchange(contrib.reshape(peers, rows, pa_width).astype(jnp.bfloat16), AB_BITS)
    return place_rows(left_list, returned, occ_count, a_parts, b_parts)


def solution(mesh):
    fine = Mesh(np.asarray(mesh.devices).reshape((2,) * len(ALL_BITS)), ALL_BITS)
    placed = (P(None, ALL_BITS, None), P(), P(), P(), P())
    return jax.shard_map(body, mesh=fine, in_specs=placed, out_specs=P(None, ALL_BITS, None), check_vma=False)
```

```python
import jax
import jax.numpy as jnp
import numpy as np
from jax import lax
from jax.experimental import pallas as pl
from jax.experimental.pallas import tpu as pltpu
from jax.sharding import Mesh, PartitionSpec as P

GRP_BITS = ("y1", "y0", "z2", "z1", "z0")
INNER_BITS = ("y2", "x2", "x1", "x0", "c")
ALL_BITS = GRP_BITS + INNER_BITS
A_BITS = ("x2", "x1", "y2", "y1")
B_BITS = ("z2", "z1")
AB_BITS = A_BITS + B_BITS
B_SUM_BITS = ("c",)
A_SUM_BITS = ("x0", "y0", "z0")
INTERPRET = False


def exchange(x, axes):
    return lax.all_to_all(x, axes, split_axis=0, concat_axis=0, tiled=True)


def pack_rows(left_list, right_occ, b_tensor, a_parts, b_parts):
    _, rows, virtuals = b_tensor.shape
    pairs = left_list.shape[0]
    a_width, b_width = virtuals // a_parts, virtuals // b_parts

    def kernel(left_ref, right_ref, b_ref, out_ref, buf, sems):
        copies = []
        for p in range(pairs + 1):
            orbital = right_ref[0] if p == pairs else left_ref[p]
            copies.append(pltpu.make_async_copy(b_ref.at[orbital], buf.at[p], sems.at[p]))
            copies[-1].start()
        for p in range(pairs):
            copies[p].wait()
            start = b_width + p * a_width
            for a in range(a_parts):
                piece = buf[p, :, a * a_width : (a + 1) * a_width]
                for b in range(b_parts):
                    out_ref[a * b_parts + b, :, start : start + a_width] = piece
        copies[pairs].wait()
        for b in range(b_parts):
            piece = buf[pairs, :, b * b_width : (b + 1) * b_width]
            for a in range(a_parts):
                out_ref[a * b_parts + b, :, :b_width] = piece

    return pl.pallas_call(
        kernel,
        out_shape=jax.ShapeDtypeStruct((a_parts * b_parts, rows, b_width + pairs * a_width), b_tensor.dtype),
        in_specs=[
            pl.BlockSpec(memory_space=pltpu.SMEM),
            pl.BlockSpec(memory_space=pltpu.SMEM),
            pl.BlockSpec(memory_space=pl.ANY),
        ],
        out_specs=pl.BlockSpec(memory_space=pltpu.VMEM),
        scratch_shapes=[pltpu.VMEM((pairs + 1, rows, virtuals), b_tensor.dtype), pltpu.SemaphoreType.DMA((pairs + 1,))],
        interpret=INTERPRET,
    )(left_list, right_occ, b_tensor)


def place_rows(left_list, returned, occ_count, a_parts, b_parts):
    _, rows, pa_width = returned.shape
    pairs = left_list.shape[0]
    a_width = pa_width // pairs
    virtuals = a_parts * a_width

    def kernel(left_ref, in_ref, out_ref, rows_ref):
        for a in range(a_parts):
            total = in_ref[a * b_parts].astype(jnp.float32)
            for b in range(1, b_parts):
                total = total + in_ref[a * b_parts + b].astype(jnp.float32)
            for p in range(pairs):
                rows_ref[p, :, a * a_width : (a + 1) * a_width] = total[:, p * a_width : (p + 1) * a_width]
        for orbital in range(occ_count):
            total = jnp.zeros((rows, virtuals), jnp.float32)
            for p in range(pairs):
                total = total + jnp.where(left_ref[p] == orbital, rows_ref[p], 0.0)
            out_ref[orbital] = total

    return pl.pallas_call(
        kernel,
        out_shape=jax.ShapeDtypeStruct((occ_count, rows, virtuals), jnp.float32),
        in_specs=[pl.BlockSpec(memory_space=pltpu.SMEM), pl.BlockSpec(memory_space=pltpu.VMEM)],
        out_specs=pl.BlockSpec(memory_space=pltpu.VMEM),
        scratch_shapes=[pltpu.VMEM((pairs, rows, virtuals), jnp.float32)],
        interpret=INTERPRET,
    )(left_list, returned)


def body(b_tensor, occ_energy, vir_energy, left_list, right_occ):
    occ_count, rows, virtuals = b_tensor.shape
    pairs = left_list.shape[0]
    a_parts, b_parts = 2 ** len(A_BITS), 2 ** len(B_BITS)
    a_subs, b_subs = 2 ** len(A_SUM_BITS), 2 ** len(B_SUM_BITS)
    a_width, b_width = virtuals // a_parts, virtuals // b_parts
    pa_width = pairs * a_width
    sub_rows, sub_cols = pa_width // a_subs, b_width // b_subs
    peers = a_parts * b_parts
    group_rows = peers * rows

    second_occ = right_occ[0]
    packed = pack_rows(left_list, right_occ, b_tensor, a_parts, b_parts)
    got = exchange(packed, AB_BITS)

    b_sub = lax.axis_index(B_SUM_BITS)
    a_rank, b_rank = lax.axis_index(A_BITS), lax.axis_index(B_BITS)
    a_sub = lax.axis_index(A_SUM_BITS)
    vir_a = lax.dynamic_slice_in_dim(vir_energy, a_rank * a_width, a_width)
    shift = occ_energy[left_list] + occ_energy[second_occ]
    row_part = (shift[:, None] - vir_a[None, :]).reshape(pa_width)
    row_part = lax.dynamic_slice_in_dim(row_part, a_sub * sub_rows, sub_rows)
    vir_b = lax.dynamic_slice_in_dim(vir_energy, b_rank * b_width + b_sub * sub_cols, sub_cols)
    got, row_part, vir_b = lax.optimization_barrier((got, row_part, vir_b))

    got = got.reshape(group_rows, b_width + pa_width)
    right = got[:, :b_width]
    left = got[:, b_width:]

    def half_of(half):
        return lax.dynamic_slice_in_dim(right, half * sub_cols, sub_cols, axis=1)

    swap = [(0, 1), (1, 0)]

    def partial_of(half):
        cols = half_of(half)
        return lax.dot_general(left, cols, (((0,), (0,)), ((), ())), preferred_element_type=jnp.float32)

    received = lax.ppermute(partial_of(1 - b_sub), B_SUM_BITS, swap)
    own = lax.optimization_barrier(partial_of(b_sub))
    paired = own + received
    shares = exchange(paired.reshape(a_subs, sub_rows, sub_cols), A_SUM_BITS).sum(axis=0)

    denominator = row_part[:, None] - vir_b[None, :]
    amp_tile = (shares / denominator).astype(jnp.bfloat16)

    amps = exchange(jnp.broadcast_to(amp_tile[None], (a_subs, sub_rows, sub_cols)), A_SUM_BITS)
    amps = amps.reshape(pa_width, sub_cols)
    other_amps = lax.ppermute(amps, B_SUM_BITS, swap)

    def contribution(cols, amp_cols):
        return lax.dot_general(cols, amp_cols, (((1,), (1,)), ((), ())), preferred_element_type=jnp.float32)

    own = lax.optimization_barrier(contribution(half_of(b_sub), amps))
    contrib = own + contribution(half_of(1 - b_sub), other_amps)
    returned = exchange(contrib.reshape(peers, rows, pa_width).astype(jnp.bfloat16), AB_BITS)
    return place_rows(left_list, returned, occ_count, a_parts, b_parts)


def solution(mesh):
    fine = Mesh(np.asarray(mesh.devices).reshape((2,) * len(ALL_BITS)), ALL_BITS)
    placed = (P(None, ALL_BITS, None), P(), P(), P(), P())
    return jax.shard_map(body, mesh=fine, in_specs=placed, out_specs=P(None, ALL_BITS, None), check_vma=False)
```

```python
import jax
import jax.numpy as jnp
import numpy as np
from jax import lax
from jax.experimental import pallas as pl
from jax.experimental.pallas import tpu as pltpu
from jax.sharding import Mesh, PartitionSpec as P

GRP_BITS = ("y1", "y0", "z2", "z1", "z0")
INNER_BITS = ("y2", "x2", "x1", "x0", "c")
ALL_BITS = GRP_BITS + INNER_BITS
A_BITS = ("x2", "x1", "y2", "y1")
B_BITS = ("z2", "z1")
B_SUM_BITS = ("c",)
A_SUM_BITS = ("x0", "y0", "z0")
INTERPRET = False


def exchange(x, axes):
    return lax.all_to_all(x, axes, split_axis=0, concat_axis=0, tiled=True)


def pick_columns(orbitals, b_tensor, parts, lanes):
    _, rows, virtuals = b_tensor.shape
    count = orbitals.shape[0]
    width = virtuals // parts

    def kernel(orbital_ref, b_ref, out_ref, buf, sems):
        copies = []
        for k in range(count):
            copies.append(pltpu.make_async_copy(b_ref.at[orbital_ref[k]], buf.at[k], sems.at[k]))
            copies[-1].start()
        for k in range(count):
            copies[k].wait()
            for part in range(parts):
                out_ref[part, :, k * width : (k + 1) * width] = buf[k, :, part * width : (part + 1) * width]
        if count * width < lanes:
            out_ref[:, :, count * width :] = jnp.zeros((parts, rows, lanes - count * width), out_ref.dtype)

    return pl.pallas_call(
        kernel,
        out_shape=jax.ShapeDtypeStruct((parts, rows, lanes), b_tensor.dtype),
        in_specs=[pl.BlockSpec(memory_space=pltpu.SMEM), pl.BlockSpec(memory_space=pl.ANY)],
        out_specs=pl.BlockSpec(memory_space=pltpu.VMEM),
        scratch_shapes=[pltpu.VMEM((count, rows, virtuals), b_tensor.dtype), pltpu.SemaphoreType.DMA((count,))],
        interpret=INTERPRET,
    )(orbitals, b_tensor)


def place_rows(left_list, returned, occ_count):
    a_parts, rows, pa_width = returned.shape
    pairs = left_list.shape[0]
    a_width = pa_width // pairs
    virtuals = a_parts * a_width

    def kernel(left_ref, in_ref, out_ref, rows_ref):
        for a in range(a_parts):
            for p in range(pairs):
                rows_ref[p, :, a * a_width : (a + 1) * a_width] = in_ref[a, :, p * a_width : (p + 1) * a_width]
        for orbital in range(occ_count):
            total = jnp.zeros((rows, virtuals), jnp.float32)
            for p in range(pairs):
                total = total + jnp.where(left_ref[p] == orbital, rows_ref[p], 0.0)
            out_ref[orbital] = total

    return pl.pallas_call(
        kernel,
        out_shape=jax.ShapeDtypeStruct((occ_count, rows, virtuals), jnp.float32),
        in_specs=[pl.BlockSpec(memory_space=pltpu.SMEM), pl.BlockSpec(memory_space=pltpu.VMEM)],
        out_specs=pl.BlockSpec(memory_space=pltpu.VMEM),
        scratch_shapes=[pltpu.VMEM((pairs, rows, virtuals), jnp.float32)],
        interpret=INTERPRET,
    )(left_list, returned)


def body(b_tensor, occ_energy, vir_energy, left_list, right_occ):
    occ_count, rows, virtuals = b_tensor.shape
    pairs = left_list.shape[0]
    a_parts, b_parts = 2 ** len(A_BITS), 2 ** len(B_BITS)
    a_subs, b_subs = 2 ** len(A_SUM_BITS), 2 ** len(B_SUM_BITS)
    a_width, b_width = virtuals // a_parts, virtuals // b_parts
    pa_width = pairs * a_width
    sub_rows, sub_cols = pa_width // a_subs, b_width // b_subs
    group_rows = a_parts * b_parts * rows

    second_occ = right_occ[0]
    right = exchange(pick_columns(right_occ, b_tensor, b_parts, b_width), B_BITS)

    b_sub = lax.axis_index(B_SUM_BITS)
    a_rank, b_rank = lax.axis_index(A_BITS), lax.axis_index(B_BITS)
    a_sub = lax.axis_index(A_SUM_BITS)
    vir_a = lax.dynamic_slice_in_dim(vir_energy, a_rank * a_width, a_width)
    shift = occ_energy[left_list] + occ_energy[second_occ]
    row_part = (shift[:, None] - vir_a[None, :]).reshape(pa_width)
    row_part = lax.dynamic_slice_in_dim(row_part, a_sub * sub_rows, sub_rows)
    vir_b = lax.dynamic_slice_in_dim(vir_energy, b_rank * b_width + b_sub * sub_cols, sub_cols)
    left = pick_columns(left_list, b_tensor, a_parts, b_width)
    right, left, row_part, vir_b = lax.optimization_barrier((right, left, row_part, vir_b))

    right = jnp.broadcast_to(right.reshape(1, b_parts * rows, b_width), (a_parts, b_parts * rows, b_width))
    got = exchange(jnp.concatenate([right, left], axis=1), A_BITS)
    right = got[:, : b_parts * rows].reshape(a_parts, b_parts, rows, b_width)
    right = right.transpose(1, 0, 2, 3).reshape(group_rows, b_width)
    left = got[:, b_parts * rows :, :pa_width].reshape(1, a_parts * rows, pa_width)
    left = exchange(jnp.broadcast_to(left, (b_parts, a_parts * rows, pa_width)), B_BITS)
    left = left.reshape(group_rows, pa_width)

    def half_of(half):
        return lax.dynamic_slice_in_dim(right, half * sub_cols, sub_cols, axis=1)

    swap = [(0, 1), (1, 0)]

    def partial_of(half):
        cols = half_of(half)
        return lax.dot_general(left, cols, (((0,), (0,)), ((), ())), preferred_element_type=jnp.float32)

    received = lax.ppermute(partial_of(1 - b_sub), B_SUM_BITS, swap)
    own = lax.optimization_barrier(partial_of(b_sub))
    paired = own + received
    shares = exchange(paired.reshape(a_subs, sub_rows, sub_cols), A_SUM_BITS).sum(axis=0)

    denominator = row_part[:, None] - vir_b[None, :]
    amp_tile = (shares / denominator).astype(jnp.bfloat16)

    amps = exchange(jnp.broadcast_to(amp_tile[None], (a_subs, sub_rows, sub_cols)), A_SUM_BITS)
    amps = amps.reshape(pa_width, sub_cols)
    other_amps = lax.ppermute(amps, B_SUM_BITS, swap)

    def contribution(cols, amp_cols):
        return lax.dot_general(cols, amp_cols, (((1,), (1,)), ((), ())), preferred_element_type=jnp.float32)

    own = lax.optimization_barrier(contribution(half_of(b_sub), amps))
    contrib = own + contribution(half_of(1 - b_sub), other_amps)
    parts = exchange(contrib.astype(jnp.bfloat16).reshape(b_parts, a_parts * rows, pa_width), B_BITS)
    returned = exchange(parts.astype(jnp.float32).sum(axis=0).reshape(a_parts, rows, pa_width), A_BITS)
    return place_rows(left_list, returned, occ_count)


def solution(mesh):
    fine = Mesh(np.asarray(mesh.devices).reshape((2,) * len(ALL_BITS)), ALL_BITS)
    placed = (P(None, ALL_BITS, None), P(), P(), P(), P())
    return jax.shard_map(body, mesh=fine, in_specs=placed, out_specs=P(None, ALL_BITS, None), check_vma=False)
```

```python
import jax
import jax.numpy as jnp
import numpy as np
from jax import lax
from jax.experimental import pallas as pl
from jax.experimental.pallas import tpu as pltpu
from jax.sharding import Mesh, PartitionSpec as P

GRP_BITS = ("y1", "y0", "z2", "z1", "z0")
INNER_BITS = ("y2", "x2", "x1", "x0", "c")
ALL_BITS = GRP_BITS + INNER_BITS
A_BITS = ("y2", "y1", "y0", "z2")
B_BITS = ("z1", "z0")
AB_BITS = A_BITS + B_BITS
B_SUM_BITS = ("c",)
A_SUM_BITS = ("x2", "x1", "x0")
INTERPRET = False


def exchange(x, axes):
    return lax.all_to_all(x, axes, split_axis=0, concat_axis=0, tiled=True)


def pack_rows(left_list, right_occ, b_tensor, a_parts, b_parts):
    _, rows, virtuals = b_tensor.shape
    pairs = left_list.shape[0]
    a_width, b_width = virtuals // a_parts, virtuals // b_parts

    def kernel(left_ref, right_ref, b_ref, out_ref, buf, sems):
        copies = []
        for p in range(pairs + 1):
            orbital = right_ref[0] if p == pairs else left_ref[p]
            copies.append(pltpu.make_async_copy(b_ref.at[orbital], buf.at[p], sems.at[p]))
            copies[-1].start()
        for p in range(pairs):
            copies[p].wait()
            start = b_width + p * a_width
            for a in range(a_parts):
                piece = buf[p, :, a * a_width : (a + 1) * a_width]
                for b in range(b_parts):
                    out_ref[a * b_parts + b, :, start : start + a_width] = piece
        copies[pairs].wait()
        for b in range(b_parts):
            piece = buf[pairs, :, b * b_width : (b + 1) * b_width]
            for a in range(a_parts):
                out_ref[a * b_parts + b, :, :b_width] = piece

    return pl.pallas_call(
        kernel,
        out_shape=jax.ShapeDtypeStruct((a_parts * b_parts, rows, b_width + pairs * a_width), b_tensor.dtype),
        in_specs=[
            pl.BlockSpec(memory_space=pltpu.SMEM),
            pl.BlockSpec(memory_space=pltpu.SMEM),
            pl.BlockSpec(memory_space=pl.ANY),
        ],
        out_specs=pl.BlockSpec(memory_space=pltpu.VMEM),
        scratch_shapes=[pltpu.VMEM((pairs + 1, rows, virtuals), b_tensor.dtype), pltpu.SemaphoreType.DMA((pairs + 1,))],
        interpret=INTERPRET,
    )(left_list, right_occ, b_tensor)


def place_rows(left_list, returned, occ_count, a_parts, b_parts):
    _, rows, pa_width = returned.shape
    pairs = left_list.shape[0]
    a_width = pa_width // pairs
    virtuals = a_parts * a_width

    def kernel(left_ref, in_ref, out_ref, rows_ref):
        for a in range(a_parts):
            total = in_ref[a * b_parts].astype(jnp.float32)
            for b in range(1, b_parts):
                total = total + in_ref[a * b_parts + b].astype(jnp.float32)
            for p in range(pairs):
                rows_ref[p, :, a * a_width : (a + 1) * a_width] = total[:, p * a_width : (p + 1) * a_width]
        for orbital in range(occ_count):
            total = jnp.zeros((rows, virtuals), jnp.float32)
            for p in range(pairs):
                total = total + jnp.where(left_ref[p] == orbital, rows_ref[p], 0.0)
            out_ref[orbital] = total

    return pl.pallas_call(
        kernel,
        out_shape=jax.ShapeDtypeStruct((occ_count, rows, virtuals), jnp.float32),
        in_specs=[pl.BlockSpec(memory_space=pltpu.SMEM), pl.BlockSpec(memory_space=pltpu.VMEM)],
        out_specs=pl.BlockSpec(memory_space=pltpu.VMEM),
        scratch_shapes=[pltpu.VMEM((pairs, rows, virtuals), jnp.float32)],
        interpret=INTERPRET,
    )(left_list, returned)


def sum_over_ring(parts):
    ring, rows, cols = parts.shape
    largest = jnp.max(jnp.abs(parts))
    exponent = jnp.clip(14.0 - jnp.ceil(jnp.log2(jnp.maximum(largest, 1e-37))), -100.0, 100.0)
    scaled = (parts * jnp.exp2(exponent)).astype(jnp.float16)
    tag = jnp.full((ring, 8, cols), exponent, jnp.float16)
    got = exchange(jnp.concatenate([scaled, tag], axis=1), A_SUM_BITS)
    undo = jnp.exp2(-got[:, rows : rows + 1].astype(jnp.float32))
    return (got[:, :rows].astype(jnp.float32) * undo).sum(axis=0)


def body(b_tensor, occ_energy, vir_energy, left_list, right_occ):
    occ_count, rows, virtuals = b_tensor.shape
    pairs = left_list.shape[0]
    a_parts, b_parts = 2 ** len(A_BITS), 2 ** len(B_BITS)
    a_subs, b_subs = 2 ** len(A_SUM_BITS), 2 ** len(B_SUM_BITS)
    a_width, b_width = virtuals // a_parts, virtuals // b_parts
    pa_width = pairs * a_width
    sub_rows, sub_cols = pa_width // a_subs, b_width // b_subs
    peers = a_parts * b_parts
    group_rows = peers * rows

    second_occ = right_occ[0]
    packed = pack_rows(left_list, right_occ, b_tensor, a_parts, b_parts)
    got = exchange(packed, AB_BITS)

    b_sub = lax.axis_index(B_SUM_BITS)
    a_rank, b_rank = lax.axis_index(A_BITS), lax.axis_index(B_BITS)
    a_sub = lax.axis_index(A_SUM_BITS)
    vir_a = lax.dynamic_slice_in_dim(vir_energy, a_rank * a_width, a_width)
    shift = occ_energy[left_list] + occ_energy[second_occ]
    row_part = (shift[:, None] - vir_a[None, :]).reshape(pa_width)
    row_part = lax.dynamic_slice_in_dim(row_part, a_sub * sub_rows, sub_rows)
    vir_b = lax.dynamic_slice_in_dim(vir_energy, b_rank * b_width + b_sub * sub_cols, sub_cols)
    got, row_part, vir_b = lax.optimization_barrier((got, row_part, vir_b))

    got = got.reshape(group_rows, b_width + pa_width)
    right = got[:, :b_width]
    left = got[:, b_width:]

    def half_of(half):
        return lax.dynamic_slice_in_dim(right, half * sub_cols, sub_cols, axis=1)

    swap = [(0, 1), (1, 0)]

    def partial_of(half):
        cols = half_of(half)
        return lax.dot_general(left, cols, (((0,), (0,)), ((), ())), preferred_element_type=jnp.float32)

    received = lax.ppermute(partial_of(1 - b_sub), B_SUM_BITS, swap)
    own = lax.optimization_barrier(partial_of(b_sub))
    paired = own + received
    shares = sum_over_ring(paired.reshape(a_subs, sub_rows, sub_cols))

    denominator = row_part[:, None] - vir_b[None, :]
    amp_tile = (shares / denominator).astype(jnp.bfloat16)

    amps = exchange(jnp.broadcast_to(amp_tile[None], (a_subs, sub_rows, sub_cols)), A_SUM_BITS)
    amps = amps.reshape(pa_width, sub_cols)
    other_amps = lax.ppermute(amps, B_SUM_BITS, swap)

    def contribution(cols, amp_cols):
        return lax.dot_general(cols, amp_cols, (((1,), (1,)), ((), ())), preferred_element_type=jnp.float32)

    own = lax.optimization_barrier(contribution(half_of(b_sub), amps))
    contrib = own + contribution(half_of(1 - b_sub), other_amps)
    returned = exchange(contrib.reshape(peers, rows, pa_width).astype(jnp.bfloat16), AB_BITS)
    return place_rows(left_list, returned, occ_count, a_parts, b_parts)


def solution(mesh):
    fine = Mesh(np.asarray(mesh.devices).reshape((2,) * len(ALL_BITS)), ALL_BITS)
    placed = (P(None, ALL_BITS, None), P(), P(), P(), P())
    return jax.shard_map(body, mesh=fine, in_specs=placed, out_specs=P(None, ALL_BITS, None), check_vma=False)
```

```python
import jax
import jax.numpy as jnp
import numpy as np
from jax import lax
from jax.experimental import pallas as pl
from jax.experimental.pallas import tpu as pltpu
from jax.sharding import Mesh, PartitionSpec as P

GRP_BITS = ("y1", "y0", "z2", "z1", "z0")
INNER_BITS = ("y2", "x2", "x1", "x0", "c")
ALL_BITS = GRP_BITS + INNER_BITS
A_BITS = ("x2", "x1", "y2", "y1")
B_BITS = ("z2", "z1")
AB_BITS = A_BITS + B_BITS
B_SUM_BITS = ("c",)
A_SUM_BITS = ("x0", "y0", "z0")
INTERPRET = False


def exchange(x, axes):
    return lax.all_to_all(x, axes, split_axis=0, concat_axis=0, tiled=True)


def pack_rows(left_list, right_occ, b_tensor, a_parts, b_parts):
    _, rows, virtuals = b_tensor.shape
    pairs = left_list.shape[0]
    a_width, b_width = virtuals // a_parts, virtuals // b_parts

    def kernel(left_ref, right_ref, b_ref, out_ref, buf, sems):
        copies = []
        for p in range(pairs + 1):
            orbital = right_ref[0] if p == pairs else left_ref[p]
            copies.append(pltpu.make_async_copy(b_ref.at[orbital], buf.at[p], sems.at[p]))
            copies[-1].start()
        for p in range(pairs):
            copies[p].wait()
            start = b_width + p * a_width
            for a in range(a_parts):
                piece = buf[p, :, a * a_width : (a + 1) * a_width]
                for b in range(b_parts):
                    out_ref[a * b_parts + b, :, start : start + a_width] = piece
        copies[pairs].wait()
        for b in range(b_parts):
            piece = buf[pairs, :, b * b_width : (b + 1) * b_width]
            for a in range(a_parts):
                out_ref[a * b_parts + b, :, :b_width] = piece

    return pl.pallas_call(
        kernel,
        out_shape=jax.ShapeDtypeStruct((a_parts * b_parts, rows, b_width + pairs * a_width), b_tensor.dtype),
        in_specs=[
            pl.BlockSpec(memory_space=pltpu.SMEM),
            pl.BlockSpec(memory_space=pltpu.SMEM),
            pl.BlockSpec(memory_space=pl.ANY),
        ],
        out_specs=pl.BlockSpec(memory_space=pltpu.VMEM),
        scratch_shapes=[pltpu.VMEM((pairs + 1, rows, virtuals), b_tensor.dtype), pltpu.SemaphoreType.DMA((pairs + 1,))],
        interpret=INTERPRET,
    )(left_list, right_occ, b_tensor)


def place_rows(left_list, returned, occ_count, a_parts, b_parts):
    _, rows, pa_width = returned.shape
    pairs = left_list.shape[0]
    a_width = pa_width // pairs
    virtuals = a_parts * a_width

    def kernel(left_ref, in_ref, out_ref, rows_ref):
        for a in range(a_parts):
            total = in_ref[a * b_parts].astype(jnp.float32)
            for b in range(1, b_parts):
                total = total + in_ref[a * b_parts + b].astype(jnp.float32)
            for p in range(pairs):
                rows_ref[p, :, a * a_width : (a + 1) * a_width] = total[:, p * a_width : (p + 1) * a_width]
        for orbital in range(occ_count):
            total = jnp.zeros((rows, virtuals), jnp.float32)
            for p in range(pairs):
                total = total + jnp.where(left_ref[p] == orbital, rows_ref[p], 0.0)
            out_ref[orbital] = total

    return pl.pallas_call(
        kernel,
        out_shape=jax.ShapeDtypeStruct((occ_count, rows, virtuals), jnp.float32),
        in_specs=[pl.BlockSpec(memory_space=pltpu.SMEM), pl.BlockSpec(memory_space=pltpu.VMEM)],
        out_specs=pl.BlockSpec(memory_space=pltpu.VMEM),
        scratch_shapes=[pltpu.VMEM((pairs, rows, virtuals), jnp.float32)],
        interpret=INTERPRET,
    )(left_list, returned)


def sum_over_cube(parts):
    cube, rows, cols = parts.shape
    largest = jnp.max(jnp.abs(parts))
    exponent = jnp.clip(14.0 - jnp.ceil(jnp.log2(jnp.maximum(largest, 1e-37))), -100.0, 100.0)
    scaled = (parts * jnp.exp2(exponent)).astype(jnp.float16)
    tag = jnp.full((cube, 8, cols), exponent, jnp.float16)
    got = exchange(jnp.concatenate([scaled, tag], axis=1), A_SUM_BITS)
    undo = jnp.exp2(-got[:, rows : rows + 1].astype(jnp.float32))
    return (got[:, :rows].astype(jnp.float32) * undo).sum(axis=0)


def body(b_tensor, occ_energy, vir_energy, left_list, right_occ):
    occ_count, rows, virtuals = b_tensor.shape
    pairs = left_list.shape[0]
    a_parts, b_parts = 2 ** len(A_BITS), 2 ** len(B_BITS)
    a_subs, b_subs = 2 ** len(A_SUM_BITS), 2 ** len(B_SUM_BITS)
    a_width, b_width = virtuals // a_parts, virtuals // b_parts
    pa_width = pairs * a_width
    sub_rows, sub_cols = pa_width // a_subs, b_width // b_subs
    peers = a_parts * b_parts
    group_rows = peers * rows

    second_occ = right_occ[0]
    packed = pack_rows(left_list, right_occ, b_tensor, a_parts, b_parts)
    got = exchange(packed, AB_BITS)

    b_sub = lax.axis_index(B_SUM_BITS)
    a_rank, b_rank = lax.axis_index(A_BITS), lax.axis_index(B_BITS)
    a_sub = lax.axis_index(A_SUM_BITS)
    vir_a = lax.dynamic_slice_in_dim(vir_energy, a_rank * a_width, a_width)
    shift = occ_energy[left_list] + occ_energy[second_occ]
    row_part = (shift[:, None] - vir_a[None, :]).reshape(pa_width)
    row_part = lax.dynamic_slice_in_dim(row_part, a_sub * sub_rows, sub_rows)
    vir_b = lax.dynamic_slice_in_dim(vir_energy, b_rank * b_width + b_sub * sub_cols, sub_cols)
    got, row_part, vir_b = lax.optimization_barrier((got, row_part, vir_b))

    got = got.reshape(group_rows, b_width + pa_width)
    right = got[:, :b_width]
    left = got[:, b_width:]

    def half_of(half):
        return lax.dynamic_slice_in_dim(right, half * sub_cols, sub_cols, axis=1)

    swap = [(0, 1), (1, 0)]

    def partial_of(half):
        cols = half_of(half)
        return lax.dot_general(left, cols, (((0,), (0,)), ((), ())), preferred_element_type=jnp.float32)

    received = lax.ppermute(partial_of(1 - b_sub), B_SUM_BITS, swap)
    own = lax.optimization_barrier(partial_of(b_sub))
    paired = own + received
    shares = sum_over_cube(paired.reshape(a_subs, sub_rows, sub_cols))

    denominator = row_part[:, None] - vir_b[None, :]
    amp_tile = (shares / denominator).astype(jnp.bfloat16)

    amps = exchange(jnp.broadcast_to(amp_tile[None], (a_subs, sub_rows, sub_cols)), A_SUM_BITS)
    amps = amps.reshape(pa_width, sub_cols)
    other_amps = lax.ppermute(amps, B_SUM_BITS, swap)

    def contribution(cols, amp_cols):
        return lax.dot_general(cols, amp_cols, (((1,), (1,)), ((), ())), preferred_element_type=jnp.float32)

    own = lax.optimization_barrier(contribution(half_of(b_sub), amps))
    contrib = own + contribution(half_of(1 - b_sub), other_amps)
    returned = exchange(contrib.reshape(peers, rows, pa_width).astype(jnp.bfloat16), AB_BITS)
    return place_rows(left_list, returned, occ_count, a_parts, b_parts)


def solution(mesh):
    fine = Mesh(np.asarray(mesh.devices).reshape((2,) * len(ALL_BITS)), ALL_BITS)
    placed = (P(None, ALL_BITS, None), P(), P(), P(), P())
    return jax.shard_map(body, mesh=fine, in_specs=placed, out_specs=P(None, ALL_BITS, None), check_vma=False)
```

```python
import jax
import jax.numpy as jnp
import numpy as np
from jax import lax
from jax.experimental import pallas as pl
from jax.experimental.pallas import tpu as pltpu
from jax.sharding import Mesh, PartitionSpec as P

GRP_BITS = ("y1", "y0", "z2", "z1", "z0")
INNER_BITS = ("y2", "x2", "x1", "x0", "c")
ALL_BITS = GRP_BITS + INNER_BITS
A_BITS = ("y2", "y1", "y0", "z2")
B_BITS = ("z1", "z0")
AB_BITS = A_BITS + B_BITS
B_SUM_BITS = ("c",)
A_SUM_BITS = ("x2", "x1", "x0")
INTERPRET = False


def exchange(x, axes):
    return lax.all_to_all(x, axes, split_axis=0, concat_axis=0, tiled=True)


def pack_rows(left_list, right_occ, b_tensor, a_parts, b_parts):
    _, rows, virtuals = b_tensor.shape
    pairs = left_list.shape[0]
    a_width, b_width = virtuals // a_parts, virtuals // b_parts

    def kernel(left_ref, right_ref, b_ref, out_ref, buf, sems):
        copies = []
        for p in range(pairs + 1):
            orbital = right_ref[0] if p == pairs else left_ref[p]
            copies.append(pltpu.make_async_copy(b_ref.at[orbital], buf.at[p], sems.at[p]))
            copies[-1].start()
        for p in range(pairs):
            copies[p].wait()
            start = b_width + p * a_width
            for a in range(a_parts):
                piece = buf[p, :, a * a_width : (a + 1) * a_width]
                for b in range(b_parts):
                    out_ref[a * b_parts + b, :, start : start + a_width] = piece
        copies[pairs].wait()
        for b in range(b_parts):
            piece = buf[pairs, :, b * b_width : (b + 1) * b_width]
            for a in range(a_parts):
                out_ref[a * b_parts + b, :, :b_width] = piece

    return pl.pallas_call(
        kernel,
        out_shape=jax.ShapeDtypeStruct((a_parts * b_parts, rows, b_width + pairs * a_width), b_tensor.dtype),
        in_specs=[
            pl.BlockSpec(memory_space=pltpu.SMEM),
            pl.BlockSpec(memory_space=pltpu.SMEM),
            pl.BlockSpec(memory_space=pl.ANY),
        ],
        out_specs=pl.BlockSpec(memory_space=pltpu.VMEM),
        scratch_shapes=[pltpu.VMEM((pairs + 1, rows, virtuals), b_tensor.dtype), pltpu.SemaphoreType.DMA((pairs + 1,))],
        interpret=INTERPRET,
    )(left_list, right_occ, b_tensor)


def place_rows(left_list, returned, occ_count, a_parts, b_parts):
    _, rows, pa_width = returned.shape
    pairs = left_list.shape[0]
    a_width = pa_width // pairs
    virtuals = a_parts * a_width

    def kernel(left_ref, in_ref, out_ref, rows_ref, made_ref, sems):
        for a in range(a_parts):
            total = in_ref[a * b_parts].astype(jnp.float32)
            for b in range(1, b_parts):
                total = total + in_ref[a * b_parts + b].astype(jnp.float32)
            for p in range(pairs):
                rows_ref[p, :, a * a_width : (a + 1) * a_width] = total[:, p * a_width : (p + 1) * a_width]
        copies = []
        for orbital in range(occ_count):
            total = jnp.zeros((rows, virtuals), jnp.float32)
            for p in range(pairs):
                total = total + jnp.where(left_ref[p] == orbital, rows_ref[p], 0.0)
            made_ref[orbital] = total
            copies.append(pltpu.make_async_copy(made_ref.at[orbital], out_ref.at[orbital], sems.at[orbital]))
            copies[-1].start()
        for copy in copies:
            copy.wait()

    return pl.pallas_call(
        kernel,
        out_shape=jax.ShapeDtypeStruct((occ_count, rows, virtuals), jnp.float32),
        in_specs=[pl.BlockSpec(memory_space=pltpu.SMEM), pl.BlockSpec(memory_space=pltpu.VMEM)],
        out_specs=pl.BlockSpec(memory_space=pl.ANY),
        scratch_shapes=[
            pltpu.VMEM((pairs, rows, virtuals), jnp.float32),
            pltpu.VMEM((occ_count, rows, virtuals), jnp.float32),
            pltpu.SemaphoreType.DMA((occ_count,)),
        ],
        interpret=INTERPRET,
    )(left_list, returned)


def make_denominator(place, left_list, right_occ, occ_energy, vir_energy, shape, a_width):
    rows, cols = shape
    pairs, virtuals = left_list.shape[0], vir_energy.shape[0]

    def kernel(place_ref, left_ref, right_ref, occ_ref, vir_ref, out_ref):
        row = place_ref[1] + lax.broadcasted_iota(jnp.int32, (rows, 1), 0)
        shift = jnp.zeros((rows, 1), jnp.float32)
        column = place_ref[0] + row
        for p in range(pairs):
            here = (row >= p * a_width) & (row < (p + 1) * a_width)
            shift = jnp.where(here, occ_ref[left_ref[p]] + occ_ref[right_ref[0]], shift)
            column = jnp.where(here, place_ref[0] + row - p * a_width, column)
        lanes = lax.broadcasted_iota(jnp.int32, (rows, virtuals), 1)
        vir_a = jnp.sum(jnp.where(lanes == column, vir_ref[...], 0.0), axis=1, keepdims=True)
        vir_b = vir_ref[:, pl.ds(pl.multiple_of(place_ref[2], 128), cols)]
        out_ref[...] = (shift - vir_a) - vir_b

    smem = pl.BlockSpec(memory_space=pltpu.SMEM)
    return pl.pallas_call(
        kernel,
        out_shape=jax.ShapeDtypeStruct(shape, jnp.float32),
        in_specs=[smem, smem, smem, smem, pl.BlockSpec(memory_space=pltpu.VMEM)],
        out_specs=pl.BlockSpec(memory_space=pltpu.VMEM),
        interpret=INTERPRET,
    )(place, left_list, right_occ, occ_energy, vir_energy.reshape(1, virtuals))


def sum_over_ring(parts):
    ring, rows, cols = parts.shape
    largest = jnp.max(jnp.abs(parts))
    exponent = jnp.clip(14.0 - jnp.ceil(jnp.log2(jnp.maximum(largest, 1e-37))), -100.0, 100.0)
    scaled = (parts * jnp.exp2(exponent)).astype(jnp.float16)
    tag = jnp.full((ring, 8, cols), exponent, jnp.float16)
    got = exchange(jnp.concatenate([scaled, tag], axis=1), A_SUM_BITS)
    undo = jnp.exp2(-got[:, rows : rows + 1].astype(jnp.float32))
    return (got[:, :rows].astype(jnp.float32) * undo).sum(axis=0)


def body(b_tensor, occ_energy, vir_energy, left_list, right_occ):
    occ_count, rows, virtuals = b_tensor.shape
    pairs = left_list.shape[0]
    a_parts, b_parts = 2 ** len(A_BITS), 2 ** len(B_BITS)
    a_subs, b_subs = 2 ** len(A_SUM_BITS), 2 ** len(B_SUM_BITS)
    a_width, b_width = virtuals // a_parts, virtuals // b_parts
    pa_width = pairs * a_width
    sub_rows, sub_cols = pa_width // a_subs, b_width // b_subs
    peers = a_parts * b_parts
    group_rows = peers * rows

    b_sub = lax.axis_index(B_SUM_BITS)
    a_rank, b_rank = lax.axis_index(A_BITS), lax.axis_index(B_BITS)
    a_sub = lax.axis_index(A_SUM_BITS)
    place = (a_rank * a_width, a_sub * sub_rows, b_rank * b_width + b_sub * sub_cols)
    own_start = (b_sub * sub_cols).astype(jnp.uint32)
    other_start = ((1 - b_sub) * sub_cols).astype(jnp.uint32)

    packed = pack_rows(left_list, right_occ, b_tensor, a_parts, b_parts)
    packed, place, own_start, other_start = lax.optimization_barrier((packed, place, own_start, other_start))
    got = exchange(packed, AB_BITS)
    got = got.reshape(group_rows, b_width + pa_width)
    right = got[:, :b_width]
    left = got[:, b_width:]

    def half_of(start):
        return lax.dynamic_slice(right, (jnp.uint32(0), start), (group_rows, sub_cols))

    swap = [(0, 1), (1, 0)]

    def partial_of(start):
        cols = half_of(start)
        return lax.dot_general(left, cols, (((0,), (0,)), ((), ())), preferred_element_type=jnp.float32)

    first = partial_of(other_start)
    received = lax.ppermute(first, B_SUM_BITS, swap)
    place, _ = lax.optimization_barrier((place, first))
    denominator = make_denominator(
        jnp.stack(place), left_list, right_occ, occ_energy, vir_energy, (sub_rows, sub_cols), a_width
    )
    own = partial_of(own_start)
    own, denominator = lax.optimization_barrier((own, denominator))
    paired = own + received
    shares = sum_over_ring(paired.reshape(a_subs, sub_rows, sub_cols))

    amp_tile = (shares / denominator).astype(jnp.bfloat16)

    amps = exchange(jnp.broadcast_to(amp_tile[None], (a_subs, sub_rows, sub_cols)), A_SUM_BITS)
    amps = amps.reshape(pa_width, sub_cols)
    other_amps = lax.ppermute(amps, B_SUM_BITS, swap)

    def contribution(cols, amp_cols):
        return lax.dot_general(cols, amp_cols, (((1,), (1,)), ((), ())), preferred_element_type=jnp.float32)

    own = lax.optimization_barrier(contribution(half_of(own_start), amps))
    contrib = own + contribution(half_of(other_start), other_amps)
    returned = exchange(contrib.reshape(peers, rows, pa_width).astype(jnp.bfloat16), AB_BITS)
    return place_rows(left_list, returned, occ_count, a_parts, b_parts)


def solution(mesh):
    fine = Mesh(np.asarray(mesh.devices).reshape((2,) * len(ALL_BITS)), ALL_BITS)
    placed = (P(None, ALL_BITS, None), P(), P(), P(), P())
    return jax.shard_map(body, mesh=fine, in_specs=placed, out_specs=P(None, ALL_BITS, None), check_vma=False)
```

```python
import jax
import jax.numpy as jnp
import numpy as np
from jax import lax
from jax.experimental import pallas as pl
from jax.experimental.pallas import tpu as pltpu
from jax.sharding import Mesh, PartitionSpec as P

GRP_BITS = ("y1", "y0", "z2", "z1", "z0")
INNER_BITS = ("y2", "x2", "x1", "x0", "c")
ALL_BITS = GRP_BITS + INNER_BITS
A_BITS = ("y2", "y1", "y0", "z2")
B_BITS = ("z1", "z0")
AB_BITS = A_BITS + B_BITS
B_SUM_BITS = ("c",)
A_SUM_BITS = ("x2", "x1", "x0")
INTERPRET = False


def exchange(x, axes):
    return lax.all_to_all(x, axes, split_axis=0, concat_axis=0, tiled=True)


def pack_rows(left_list, right_occ, b_tensor, a_parts, b_parts):
    _, rows, virtuals = b_tensor.shape
    pairs = left_list.shape[0]
    a_width, b_width = virtuals // a_parts, virtuals // b_parts

    def kernel(left_ref, right_ref, b_ref, out_ref, buf, sems):
        copies = []
        for p in range(pairs + 1):
            orbital = right_ref[0] if p == pairs else left_ref[p]
            copies.append(pltpu.make_async_copy(b_ref.at[orbital], buf.at[p], sems.at[p]))
            copies[-1].start()
        for p in range(pairs):
            copies[p].wait()
            start = b_width + p * a_width
            for a in range(a_parts):
                piece = buf[p, :, a * a_width : (a + 1) * a_width]
                for b in range(b_parts):
                    out_ref[a * b_parts + b, :, start : start + a_width] = piece
        copies[pairs].wait()
        for b in range(b_parts):
            piece = buf[pairs, :, b * b_width : (b + 1) * b_width]
            for a in range(a_parts):
                out_ref[a * b_parts + b, :, :b_width] = piece

    return pl.pallas_call(
        kernel,
        out_shape=pltpu.VMEM((a_parts * b_parts, rows, b_width + pairs * a_width), b_tensor.dtype),
        in_specs=[
            pl.BlockSpec(memory_space=pltpu.SMEM),
            pl.BlockSpec(memory_space=pltpu.SMEM),
            pl.BlockSpec(memory_space=pl.ANY),
        ],
        out_specs=pl.BlockSpec(memory_space=pltpu.VMEM),
        scratch_shapes=[pltpu.VMEM((pairs + 1, rows, virtuals), b_tensor.dtype), pltpu.SemaphoreType.DMA((pairs + 1,))],
        interpret=INTERPRET,
    )(left_list, right_occ, b_tensor)


def place_rows(left_list, returned, occ_count, a_parts, b_parts):
    _, rows, pa_width = returned.shape
    pairs = left_list.shape[0]
    a_width = pa_width // pairs
    virtuals = a_parts * a_width

    def kernel(left_ref, in_ref, out_ref, rows_ref, made_ref, sems):
        for a in range(a_parts):
            total = in_ref[a * b_parts].astype(jnp.float32)
            for b in range(1, b_parts):
                total = total + in_ref[a * b_parts + b].astype(jnp.float32)
            for p in range(pairs):
                rows_ref[p, :, a * a_width : (a + 1) * a_width] = total[:, p * a_width : (p + 1) * a_width]
        copies = []
        for orbital in range(occ_count):
            total = jnp.zeros((rows, virtuals), jnp.float32)
            for p in range(pairs):
                total = total + jnp.where(left_ref[p] == orbital, rows_ref[p], 0.0)
            made_ref[orbital] = total
            copies.append(pltpu.make_async_copy(made_ref.at[orbital], out_ref.at[orbital], sems.at[orbital]))
            copies[-1].start()
        for copy in copies:
            copy.wait()

    return pl.pallas_call(
        kernel,
        out_shape=jax.ShapeDtypeStruct((occ_count, rows, virtuals), jnp.float32),
        in_specs=[pl.BlockSpec(memory_space=pltpu.SMEM), pl.BlockSpec(memory_space=pltpu.VMEM)],
        out_specs=pl.BlockSpec(memory_space=pl.ANY),
        scratch_shapes=[
            pltpu.VMEM((pairs, rows, virtuals), jnp.float32),
            pltpu.VMEM((occ_count, rows, virtuals), jnp.float32),
            pltpu.SemaphoreType.DMA((occ_count,)),
        ],
        interpret=INTERPRET,
    )(left_list, returned)


def make_denominator(place, left_list, right_occ, occ_energy, vir_energy, shape, a_width):
    rows, cols = shape
    pairs, virtuals = left_list.shape[0], vir_energy.shape[0]

    def kernel(place_ref, left_ref, right_ref, occ_ref, vir_ref, out_ref):
        row = place_ref[1] + lax.broadcasted_iota(jnp.int32, (rows, 1), 0)
        shift = jnp.zeros((rows, 1), jnp.float32)
        column = place_ref[0] + row
        for p in range(pairs):
            here = (row >= p * a_width) & (row < (p + 1) * a_width)
            shift = jnp.where(here, occ_ref[left_ref[p]] + occ_ref[right_ref[0]], shift)
            column = jnp.where(here, place_ref[0] + row - p * a_width, column)
        lanes = lax.broadcasted_iota(jnp.int32, (rows, virtuals), 1)
        vir_a = jnp.sum(jnp.where(lanes == column, vir_ref[...], 0.0), axis=1, keepdims=True)
        vir_b = vir_ref[:, pl.ds(pl.multiple_of(place_ref[2], 128), cols)]
        out_ref[...] = (shift - vir_a) - vir_b

    smem = pl.BlockSpec(memory_space=pltpu.SMEM)
    return pl.pallas_call(
        kernel,
        out_shape=jax.ShapeDtypeStruct(shape, jnp.float32),
        in_specs=[smem, smem, smem, smem, pl.BlockSpec(memory_space=pltpu.VMEM)],
        out_specs=pl.BlockSpec(memory_space=pltpu.VMEM),
        interpret=INTERPRET,
    )(place, left_list, right_occ, occ_energy, vir_energy.reshape(1, virtuals))


def sum_over_ring(parts):
    ring, rows, cols = parts.shape
    largest = jnp.max(jnp.abs(parts))
    exponent = jnp.clip(14.0 - jnp.ceil(jnp.log2(jnp.maximum(largest, 1e-37))), -100.0, 100.0)
    scaled = (parts * jnp.exp2(exponent)).astype(jnp.float16)
    tag = jnp.full((ring, 8, cols), exponent, jnp.float16)
    got = exchange(jnp.concatenate([scaled, tag], axis=1), A_SUM_BITS)
    undo = jnp.exp2(-got[:, rows : rows + 1].astype(jnp.float32))
    return (got[:, :rows].astype(jnp.float32) * undo).sum(axis=0)


def body(b_tensor, occ_energy, vir_energy, left_list, right_occ):
    occ_count, rows, virtuals = b_tensor.shape
    pairs = left_list.shape[0]
    a_parts, b_parts = 2 ** len(A_BITS), 2 ** len(B_BITS)
    a_subs, b_subs = 2 ** len(A_SUM_BITS), 2 ** len(B_SUM_BITS)
    a_width, b_width = virtuals // a_parts, virtuals // b_parts
    pa_width = pairs * a_width
    sub_rows, sub_cols = pa_width // a_subs, b_width // b_subs
    peers = a_parts * b_parts
    group_rows = peers * rows

    b_sub = lax.axis_index(B_SUM_BITS)
    a_rank, b_rank = lax.axis_index(A_BITS), lax.axis_index(B_BITS)
    a_sub = lax.axis_index(A_SUM_BITS)
    place = (a_rank * a_width, a_sub * sub_rows, b_rank * b_width + b_sub * sub_cols)
    own_start = (b_sub * sub_cols).astype(jnp.uint32)
    other_start = ((1 - b_sub) * sub_cols).astype(jnp.uint32)

    packed = pack_rows(left_list, right_occ, b_tensor, a_parts, b_parts)
    packed, place, own_start, other_start = lax.optimization_barrier((packed, place, own_start, other_start))
    got = exchange(packed, AB_BITS)
    got = got.reshape(group_rows, b_width + pa_width)
    right = got[:, :b_width]
    left = got[:, b_width:]

    def half_of(start):
        return lax.dynamic_slice(right, (jnp.uint32(0), start), (group_rows, sub_cols))

    swap = [(0, 1), (1, 0)]

    def partial_of(start):
        cols = half_of(start)
        return lax.dot_general(left, cols, (((0,), (0,)), ((), ())), preferred_element_type=jnp.float32)

    first = partial_of(other_start)
    received = lax.ppermute(first, B_SUM_BITS, swap)
    place, _ = lax.optimization_barrier((place, first))
    denominator = make_denominator(
        jnp.stack(place), left_list, right_occ, occ_energy, vir_energy, (sub_rows, sub_cols), a_width
    )
    own = partial_of(own_start)
    own, denominator = lax.optimization_barrier((own, denominator))
    paired = own + received
    shares = sum_over_ring(paired.reshape(a_subs, sub_rows, sub_cols))

    amp_tile = (shares / denominator).astype(jnp.bfloat16)

    amps = exchange(jnp.broadcast_to(amp_tile[None], (a_subs, sub_rows, sub_cols)), A_SUM_BITS)
    amps = amps.reshape(pa_width, sub_cols)
    other_amps = lax.ppermute(amps, B_SUM_BITS, swap)

    def contribution(cols, amp_cols):
        return lax.dot_general(cols, amp_cols, (((1,), (1,)), ((), ())), preferred_element_type=jnp.float32)

    own = lax.optimization_barrier(contribution(half_of(own_start), amps))
    contrib = own + contribution(half_of(other_start), other_amps)
    returned = exchange(contrib.reshape(peers, rows, pa_width).astype(jnp.bfloat16), AB_BITS)
    returned = pltpu.with_memory_space_constraint(returned, pltpu.VMEM)
    return place_rows(left_list, returned, occ_count, a_parts, b_parts)


def solution(mesh):
    fine = Mesh(np.asarray(mesh.devices).reshape((2,) * len(ALL_BITS)), ALL_BITS)
    placed = (P(None, ALL_BITS, None), P(), P(), P(), P())
    return jax.shard_map(body, mesh=fine, in_specs=placed, out_specs=P(None, ALL_BITS, None), check_vma=False)
```

```python
import jax
import jax.numpy as jnp
import numpy as np
from jax import lax
from jax.experimental import pallas as pl
from jax.experimental.pallas import tpu as pltpu
from jax.sharding import Mesh, PartitionSpec as P

GRP_BITS = ("y1", "y0", "z2", "z1", "z0")
INNER_BITS = ("y2", "x2", "x1", "x0", "c")
ALL_BITS = GRP_BITS + INNER_BITS
A_BITS = ("y2", "y1", "y0", "z2")
B_BITS = ("z1", "z0")
AB_BITS = A_BITS + B_BITS
B_SUM_BITS = ("c",)
A_SUM_BITS = ("x2", "x1", "x0")
INTERPRET = False


def exchange(x, axes):
    return lax.all_to_all(x, axes, split_axis=0, concat_axis=0, tiled=True)


def pack_rows(left_list, right_occ, b_tensor, a_parts, b_parts):
    _, rows, virtuals = b_tensor.shape
    pairs = left_list.shape[0]
    a_width, b_width = virtuals // a_parts, virtuals // b_parts

    def kernel(left_ref, right_ref, b_ref, out_ref, buf, sems):
        copies = []
        for p in range(pairs + 1):
            orbital = right_ref[0] if p == pairs else left_ref[p]
            copies.append(pltpu.make_async_copy(b_ref.at[orbital], buf.at[p], sems.at[p]))
            copies[-1].start()
        for p in range(pairs):
            copies[p].wait()
            start = b_width + p * a_width
            for a in range(a_parts):
                piece = buf[p, :, a * a_width : (a + 1) * a_width]
                for b in range(b_parts):
                    out_ref[a * b_parts + b, :, start : start + a_width] = piece
        copies[pairs].wait()
        for b in range(b_parts):
            piece = buf[pairs, :, b * b_width : (b + 1) * b_width]
            for a in range(a_parts):
                out_ref[a * b_parts + b, :, :b_width] = piece

    return pl.pallas_call(
        kernel,
        out_shape=jax.ShapeDtypeStruct((a_parts * b_parts, rows, b_width + pairs * a_width), b_tensor.dtype),
        in_specs=[
            pl.BlockSpec(memory_space=pltpu.SMEM),
            pl.BlockSpec(memory_space=pltpu.SMEM),
            pl.BlockSpec(memory_space=pl.ANY),
        ],
        out_specs=pl.BlockSpec(memory_space=pltpu.VMEM),
        scratch_shapes=[pltpu.VMEM((pairs + 1, rows, virtuals), b_tensor.dtype), pltpu.SemaphoreType.DMA((pairs + 1,))],
        interpret=INTERPRET,
    )(left_list, right_occ, b_tensor)


def place_rows(left_list, returned, occ_count, a_parts, b_parts):
    _, rows, pa_width = returned.shape
    pairs = left_list.shape[0]
    a_width = pa_width // pairs
    virtuals = a_parts * a_width

    def kernel(left_ref, in_ref, out_ref, rows_ref, made_ref, sems):
        for a in range(a_parts):
            total = in_ref[a * b_parts].astype(jnp.float32)
            for b in range(1, b_parts):
                total = total + in_ref[a * b_parts + b].astype(jnp.float32)
            for p in range(pairs):
                rows_ref[p, :, a * a_width : (a + 1) * a_width] = total[:, p * a_width : (p + 1) * a_width]
        copies = []
        for orbital in range(occ_count):
            total = jnp.zeros((rows, virtuals), jnp.float32)
            for p in range(pairs):
                total = total + jnp.where(left_ref[p] == orbital, rows_ref[p], 0.0)
            made_ref[orbital] = total
            copies.append(pltpu.make_async_copy(made_ref.at[orbital], out_ref.at[orbital], sems.at[orbital]))
            copies[-1].start()
        for copy in copies:
            copy.wait()

    return pl.pallas_call(
        kernel,
        out_shape=jax.ShapeDtypeStruct((occ_count, rows, virtuals), jnp.float32),
        in_specs=[pl.BlockSpec(memory_space=pltpu.SMEM), pl.BlockSpec(memory_space=pltpu.VMEM)],
        out_specs=pl.BlockSpec(memory_space=pl.ANY),
        scratch_shapes=[
            pltpu.VMEM((pairs, rows, virtuals), jnp.float32),
            pltpu.VMEM((occ_count, rows, virtuals), jnp.float32),
            pltpu.SemaphoreType.DMA((occ_count,)),
        ],
        interpret=INTERPRET,
    )(left_list, returned)


def sum_over_ring(parts):
    ring, rows, cols = parts.shape
    largest = jnp.max(jnp.abs(parts), axis=(0, 1))
    exponent = jnp.clip(14.0 - jnp.ceil(jnp.log2(jnp.maximum(largest, 1e-37))), -100.0, 100.0)
    scaled = (parts * jnp.exp2(exponent)).astype(jnp.float16)
    tag = jnp.broadcast_to(exponent.astype(jnp.float16), (ring, 8, cols))
    got = exchange(jnp.concatenate([scaled, tag], axis=1), A_SUM_BITS)
    undo = jnp.exp2(-got[:, rows : rows + 1].astype(jnp.float32))
    return (got[:, :rows].astype(jnp.float32) * undo).sum(axis=0)


def body(b_tensor, occ_energy, vir_energy, left_list, right_occ):
    occ_count, rows, virtuals = b_tensor.shape
    pairs = left_list.shape[0]
    a_parts, b_parts = 2 ** len(A_BITS), 2 ** len(B_BITS)
    a_subs, b_subs = 2 ** len(A_SUM_BITS), 2 ** len(B_SUM_BITS)
    a_width, b_width = virtuals // a_parts, virtuals // b_parts
    pa_width = pairs * a_width
    sub_rows, sub_cols = pa_width // a_subs, b_width // b_subs
    peers = a_parts * b_parts
    group_rows = peers * rows

    second_occ = right_occ[0]
    packed = pack_rows(left_list, right_occ, b_tensor, a_parts, b_parts)
    got = exchange(packed, AB_BITS)

    b_sub = lax.axis_index(B_SUM_BITS)
    a_rank, b_rank = lax.axis_index(A_BITS), lax.axis_index(B_BITS)
    a_sub = lax.axis_index(A_SUM_BITS)
    vir_a = lax.dynamic_slice_in_dim(vir_energy, a_rank * a_width, a_width)
    shift = occ_energy[left_list] + occ_energy[second_occ]
    row_part = (shift[:, None] - vir_a[None, :]).reshape(pa_width)
    row_part = lax.dynamic_slice_in_dim(row_part, a_sub * sub_rows, sub_rows)
    vir_b = lax.dynamic_slice_in_dim(vir_energy, b_rank * b_width + b_sub * sub_cols, sub_cols)
    got, row_part, vir_b = lax.optimization_barrier((got, row_part, vir_b))

    got = got.reshape(group_rows, b_width + pa_width)
    right = got[:, :b_width]
    left = got[:, b_width:]

    def half_of(half):
        return lax.dynamic_slice_in_dim(right, half * sub_cols, sub_cols, axis=1)

    swap = [(0, 1), (1, 0)]

    def partial_of(half):
        cols = half_of(half)
        return lax.dot_general(left, cols, (((0,), (0,)), ((), ())), preferred_element_type=jnp.float32)

    received = lax.ppermute(partial_of(1 - b_sub), B_SUM_BITS, swap)
    own = lax.optimization_barrier(partial_of(b_sub))
    paired = own + received
    shares = sum_over_ring(paired.reshape(a_subs, sub_rows, sub_cols))

    denominator = row_part[:, None] - vir_b[None, :]
    amp_tile = (shares / denominator).astype(jnp.bfloat16)

    amps = exchange(jnp.broadcast_to(amp_tile[None], (a_subs, sub_rows, sub_cols)), A_SUM_BITS)
    amps = amps.reshape(pa_width, sub_cols)
    other_amps = lax.ppermute(amps, B_SUM_BITS, swap)

    def contribution(cols, amp_cols):
        return lax.dot_general(cols, amp_cols, (((1,), (1,)), ((), ())), preferred_element_type=jnp.float32)

    own = lax.optimization_barrier(contribution(half_of(b_sub), amps))
    contrib = own + contribution(half_of(1 - b_sub), other_amps)
    returned = exchange(contrib.reshape(peers, rows, pa_width).astype(jnp.bfloat16), AB_BITS)
    returned = pltpu.with_memory_space_constraint(returned, pltpu.VMEM)
    return place_rows(left_list, returned, occ_count, a_parts, b_parts)


def solution(mesh):
    fine = Mesh(np.asarray(mesh.devices).reshape((2,) * len(ALL_BITS)), ALL_BITS)
    placed = (P(None, ALL_BITS, None), P(), P(), P(), P())
    return jax.shard_map(body, mesh=fine, in_specs=placed, out_specs=P(None, ALL_BITS, None), check_vma=False)
```

```python
import jax
import jax.numpy as jnp
import numpy as np
from jax import lax
from jax.experimental import pallas as pl
from jax.experimental.pallas import tpu as pltpu
from jax.sharding import Mesh, PartitionSpec as P

GRP_BITS = ("y1", "y0", "z2", "z1", "z0")
INNER_BITS = ("y2", "x2", "x1", "x0", "c")
ALL_BITS = GRP_BITS + INNER_BITS
A_BITS = ("y2", "z2", "y1", "z1")
B_BITS = ("y0", "z0")
AB_BITS = A_BITS + B_BITS
B_SUM_BITS = ("c",)
A_SUM_BITS = ("x2", "x1", "x0")
INTERPRET = False


def exchange(x, axes):
    return lax.all_to_all(x, axes, split_axis=0, concat_axis=0, tiled=True)


def pack_rows(left_list, right_occ, b_tensor, a_parts, b_parts):
    _, rows, virtuals = b_tensor.shape
    pairs = left_list.shape[0]
    a_width, b_width = virtuals // a_parts, virtuals // b_parts

    def kernel(left_ref, right_ref, b_ref, out_ref, buf, sems):
        copies = []
        for p in range(pairs + 1):
            orbital = right_ref[0] if p == pairs else left_ref[p]
            copies.append(pltpu.make_async_copy(b_ref.at[orbital], buf.at[p], sems.at[p]))
            copies[-1].start()
        for p in range(pairs):
            copies[p].wait()
            start = b_width + p * a_width
            for a in range(a_parts):
                piece = buf[p, :, a * a_width : (a + 1) * a_width]
                for b in range(b_parts):
                    out_ref[a * b_parts + b, :, start : start + a_width] = piece
        copies[pairs].wait()
        for b in range(b_parts):
            piece = buf[pairs, :, b * b_width : (b + 1) * b_width]
            for a in range(a_parts):
                out_ref[a * b_parts + b, :, :b_width] = piece

    return pl.pallas_call(
        kernel,
        out_shape=jax.ShapeDtypeStruct((a_parts * b_parts, rows, b_width + pairs * a_width), b_tensor.dtype),
        in_specs=[
            pl.BlockSpec(memory_space=pltpu.SMEM),
            pl.BlockSpec(memory_space=pltpu.SMEM),
            pl.BlockSpec(memory_space=pl.ANY),
        ],
        out_specs=pl.BlockSpec(memory_space=pltpu.VMEM),
        scratch_shapes=[pltpu.VMEM((pairs + 1, rows, virtuals), b_tensor.dtype), pltpu.SemaphoreType.DMA((pairs + 1,))],
        interpret=INTERPRET,
    )(left_list, right_occ, b_tensor)


def place_rows(left_list, returned, occ_count, a_parts, b_parts):
    _, rows, pa_width = returned.shape
    pairs = left_list.shape[0]
    a_width = pa_width // pairs
    virtuals = a_parts * a_width

    def kernel(left_ref, in_ref, out_ref, rows_ref, made_ref, sems):
        for a in range(a_parts):
            total = in_ref[a * b_parts].astype(jnp.float32)
            for b in range(1, b_parts):
                total = total + in_ref[a * b_parts + b].astype(jnp.float32)
            for p in range(pairs):
                rows_ref[p, :, a * a_width : (a + 1) * a_width] = total[:, p * a_width : (p + 1) * a_width]
        copies = []
        for orbital in range(occ_count):
            total = jnp.zeros((rows, virtuals), jnp.float32)
            for p in range(pairs):
                total = total + jnp.where(left_ref[p] == orbital, rows_ref[p], 0.0)
            made_ref[orbital] = total
            copies.append(pltpu.make_async_copy(made_ref.at[orbital], out_ref.at[orbital], sems.at[orbital]))
            copies[-1].start()
        for copy in copies:
            copy.wait()

    return pl.pallas_call(
        kernel,
        out_shape=jax.ShapeDtypeStruct((occ_count, rows, virtuals), jnp.float32),
        in_specs=[pl.BlockSpec(memory_space=pltpu.SMEM), pl.BlockSpec(memory_space=pltpu.VMEM)],
        out_specs=pl.BlockSpec(memory_space=pl.ANY),
        scratch_shapes=[
            pltpu.VMEM((pairs, rows, virtuals), jnp.float32),
            pltpu.VMEM((occ_count, rows, virtuals), jnp.float32),
            pltpu.SemaphoreType.DMA((occ_count,)),
        ],
        interpret=INTERPRET,
    )(left_list, returned)


def sum_over_ring(parts):
    ring, rows, cols = parts.shape
    largest = jnp.max(jnp.abs(parts), axis=(0, 1))
    exponent = jnp.clip(14.0 - jnp.ceil(jnp.log2(jnp.maximum(largest, 1e-37))), -100.0, 100.0)
    scaled = (parts * jnp.exp2(exponent)).astype(jnp.float16)
    tag = jnp.broadcast_to(exponent.astype(jnp.float16), (ring, 8, cols))
    got = exchange(jnp.concatenate([scaled, tag], axis=1), A_SUM_BITS)
    undo = jnp.exp2(-got[:, rows : rows + 1].astype(jnp.float32))
    return (got[:, :rows].astype(jnp.float32) * undo).sum(axis=0)


def body(b_tensor, occ_energy, vir_energy, left_list, right_occ):
    occ_count, rows, virtuals = b_tensor.shape
    pairs = left_list.shape[0]
    a_parts, b_parts = 2 ** len(A_BITS), 2 ** len(B_BITS)
    a_subs, b_subs = 2 ** len(A_SUM_BITS), 2 ** len(B_SUM_BITS)
    a_width, b_width = virtuals // a_parts, virtuals // b_parts
    pa_width = pairs * a_width
    sub_rows, sub_cols = pa_width // a_subs, b_width // b_subs
    peers = a_parts * b_parts
    group_rows = peers * rows

    second_occ = right_occ[0]
    packed = pack_rows(left_list, right_occ, b_tensor, a_parts, b_parts)
    got = exchange(packed, AB_BITS)

    b_sub = lax.axis_index(B_SUM_BITS)
    a_rank, b_rank = lax.axis_index(A_BITS), lax.axis_index(B_BITS)
    a_sub = lax.axis_index(A_SUM_BITS)
    vir_a = lax.dynamic_slice_in_dim(vir_energy, a_rank * a_width, a_width)
    shift = occ_energy[left_list] + occ_energy[second_occ]
    row_part = (shift[:, None] - vir_a[None, :]).reshape(pa_width)
    row_part = lax.dynamic_slice_in_dim(row_part, a_sub * sub_rows, sub_rows)
    vir_b = lax.dynamic_slice_in_dim(vir_energy, b_rank * b_width + b_sub * sub_cols, sub_cols)
    got, row_part, vir_b = lax.optimization_barrier((got, row_part, vir_b))

    got = got.reshape(group_rows, b_width + pa_width)
    right = got[:, :b_width]
    left = got[:, b_width:]

    def half_of(half):
        return lax.dynamic_slice_in_dim(right, half * sub_cols, sub_cols, axis=1)

    swap = [(0, 1), (1, 0)]

    def partial_of(half):
        cols = half_of(half)
        return lax.dot_general(left, cols, (((0,), (0,)), ((), ())), preferred_element_type=jnp.float32)

    received = lax.ppermute(partial_of(1 - b_sub), B_SUM_BITS, swap)
    own = lax.optimization_barrier(partial_of(b_sub))
    paired = own + received
    shares = sum_over_ring(paired.reshape(a_subs, sub_rows, sub_cols))

    denominator = row_part[:, None] - vir_b[None, :]
    amp_tile = (shares / denominator).astype(jnp.bfloat16)

    amps = exchange(jnp.broadcast_to(amp_tile[None], (a_subs, sub_rows, sub_cols)), A_SUM_BITS)
    amps = amps.reshape(pa_width, sub_cols)
    other_amps = lax.ppermute(amps, B_SUM_BITS, swap)

    def contribution(cols, amp_cols):
        return lax.dot_general(cols, amp_cols, (((1,), (1,)), ((), ())), preferred_element_type=jnp.float32)

    own = lax.optimization_barrier(contribution(half_of(b_sub), amps))
    contrib = own + contribution(half_of(1 - b_sub), other_amps)
    returned = exchange(contrib.reshape(peers, rows, pa_width).astype(jnp.bfloat16), AB_BITS)
    returned = pltpu.with_memory_space_constraint(returned, pltpu.VMEM)
    return place_rows(left_list, returned, occ_count, a_parts, b_parts)


def solution(mesh):
    fine = Mesh(np.asarray(mesh.devices).reshape((2,) * len(ALL_BITS)), ALL_BITS)
    placed = (P(None, ALL_BITS, None), P(), P(), P(), P())
    return jax.shard_map(body, mesh=fine, in_specs=placed, out_specs=P(None, ALL_BITS, None), check_vma=False)
```

```python
import jax
import jax.numpy as jnp
import numpy as np
from jax import lax
from jax.experimental import pallas as pl
from jax.experimental.pallas import tpu as pltpu
from jax.sharding import Mesh, PartitionSpec as P

GRP_BITS = ("y1", "y0", "z2", "z1", "z0")
INNER_BITS = ("y2", "x2", "x1", "x0", "c")
ALL_BITS = GRP_BITS + INNER_BITS
A_BITS = ("z2", "z1", "z0", "y2")
B_BITS = ("y1", "y0")
AB_BITS = A_BITS + B_BITS
B_SUM_BITS = ("c",)
A_SUM_BITS = ("x2", "x1", "x0")
INTERPRET = False


def exchange(x, axes):
    return lax.all_to_all(x, axes, split_axis=0, concat_axis=0, tiled=True)


def pack_rows(left_list, right_occ, b_tensor, a_parts, b_parts):
    _, rows, virtuals = b_tensor.shape
    pairs = left_list.shape[0]
    a_width, b_width = virtuals // a_parts, virtuals // b_parts

    def kernel(left_ref, right_ref, b_ref, out_ref, buf, sems):
        copies = []
        for p in range(pairs + 1):
            orbital = right_ref[0] if p == pairs else left_ref[p]
            copies.append(pltpu.make_async_copy(b_ref.at[orbital], buf.at[p], sems.at[p]))
            copies[-1].start()
        for p in range(pairs):
            copies[p].wait()
            start = b_width + p * a_width
            for a in range(a_parts):
                piece = buf[p, :, a * a_width : (a + 1) * a_width]
                for b in range(b_parts):
                    out_ref[a * b_parts + b, :, start : start + a_width] = piece
        copies[pairs].wait()
        for b in range(b_parts):
            piece = buf[pairs, :, b * b_width : (b + 1) * b_width]
            for a in range(a_parts):
                out_ref[a * b_parts + b, :, :b_width] = piece

    return pl.pallas_call(
        kernel,
        out_shape=jax.ShapeDtypeStruct((a_parts * b_parts, rows, b_width + pairs * a_width), b_tensor.dtype),
        in_specs=[
            pl.BlockSpec(memory_space=pltpu.SMEM),
            pl.BlockSpec(memory_space=pltpu.SMEM),
            pl.BlockSpec(memory_space=pl.ANY),
        ],
        out_specs=pl.BlockSpec(memory_space=pltpu.VMEM),
        scratch_shapes=[pltpu.VMEM((pairs + 1, rows, virtuals), b_tensor.dtype), pltpu.SemaphoreType.DMA((pairs + 1,))],
        interpret=INTERPRET,
    )(left_list, right_occ, b_tensor)


def place_rows(left_list, returned, occ_count, a_parts, b_parts):
    _, rows, pa_width = returned.shape
    pairs = left_list.shape[0]
    a_width = pa_width // pairs
    virtuals = a_parts * a_width

    def kernel(left_ref, in_ref, out_ref, rows_ref, made_ref, sems):
        for a in range(a_parts):
            total = in_ref[a * b_parts].astype(jnp.float32)
            for b in range(1, b_parts):
                total = total + in_ref[a * b_parts + b].astype(jnp.float32)
            for p in range(pairs):
                rows_ref[p, :, a * a_width : (a + 1) * a_width] = total[:, p * a_width : (p + 1) * a_width]
        copies = []
        for orbital in range(occ_count):
            total = jnp.zeros((rows, virtuals), jnp.float32)
            for p in range(pairs):
                total = total + jnp.where(left_ref[p] == orbital, rows_ref[p], 0.0)
            made_ref[orbital] = total
            copies.append(pltpu.make_async_copy(made_ref.at[orbital], out_ref.at[orbital], sems.at[orbital]))
            copies[-1].start()
        for copy in copies:
            copy.wait()

    return pl.pallas_call(
        kernel,
        out_shape=jax.ShapeDtypeStruct((occ_count, rows, virtuals), jnp.float32),
        in_specs=[pl.BlockSpec(memory_space=pltpu.SMEM), pl.BlockSpec(memory_space=pltpu.VMEM)],
        out_specs=pl.BlockSpec(memory_space=pl.ANY),
        scratch_shapes=[
            pltpu.VMEM((pairs, rows, virtuals), jnp.float32),
            pltpu.VMEM((occ_count, rows, virtuals), jnp.float32),
            pltpu.SemaphoreType.DMA((occ_count,)),
        ],
        interpret=INTERPRET,
    )(left_list, returned)


def sum_over_ring(parts):
    ring, rows, cols = parts.shape
    largest = jnp.max(jnp.abs(parts), axis=(0, 1))
    exponent = jnp.clip(14.0 - jnp.ceil(jnp.log2(jnp.maximum(largest, 1e-37))), -100.0, 100.0)
    scaled = (parts * jnp.exp2(exponent)).astype(jnp.float16)
    tag = jnp.broadcast_to(exponent.astype(jnp.float16), (ring, 8, cols))
    got = exchange(jnp.concatenate([scaled, tag], axis=1), A_SUM_BITS)
    undo = jnp.exp2(-got[:, rows : rows + 1].astype(jnp.float32))
    return (got[:, :rows].astype(jnp.float32) * undo).sum(axis=0)


def body(b_tensor, occ_energy, vir_energy, left_list, right_occ):
    occ_count, rows, virtuals = b_tensor.shape
    pairs = left_list.shape[0]
    a_parts, b_parts = 2 ** len(A_BITS), 2 ** len(B_BITS)
    a_subs, b_subs = 2 ** len(A_SUM_BITS), 2 ** len(B_SUM_BITS)
    a_width, b_width = virtuals // a_parts, virtuals // b_parts
    pa_width = pairs * a_width
    sub_rows, sub_cols = pa_width // a_subs, b_width // b_subs
    peers = a_parts * b_parts
    group_rows = peers * rows

    second_occ = right_occ[0]
    packed = pack_rows(left_list, right_occ, b_tensor, a_parts, b_parts)
    got = exchange(packed, AB_BITS)

    b_sub = lax.axis_index(B_SUM_BITS)
    a_rank, b_rank = lax.axis_index(A_BITS), lax.axis_index(B_BITS)
    a_sub = lax.axis_index(A_SUM_BITS)
    vir_a = lax.dynamic_slice_in_dim(vir_energy, a_rank * a_width, a_width)
    shift = occ_energy[left_list] + occ_energy[second_occ]
    row_part = (shift[:, None] - vir_a[None, :]).reshape(pa_width)
    row_part = lax.dynamic_slice_in_dim(row_part, a_sub * sub_rows, sub_rows)
    vir_b = lax.dynamic_slice_in_dim(vir_energy, b_rank * b_width + b_sub * sub_cols, sub_cols)
    got, row_part, vir_b = lax.optimization_barrier((got, row_part, vir_b))

    got = got.reshape(group_rows, b_width + pa_width)
    right = got[:, :b_width]
    left = got[:, b_width:]

    def half_of(half):
        return lax.dynamic_slice_in_dim(right, half * sub_cols, sub_cols, axis=1)

    swap = [(0, 1), (1, 0)]

    def partial_of(half):
        cols = half_of(half)
        return lax.dot_general(left, cols, (((0,), (0,)), ((), ())), preferred_element_type=jnp.float32)

    received = lax.ppermute(partial_of(1 - b_sub), B_SUM_BITS, swap)
    own = lax.optimization_barrier(partial_of(b_sub))
    paired = own + received
    shares = sum_over_ring(paired.reshape(a_subs, sub_rows, sub_cols))

    denominator = row_part[:, None] - vir_b[None, :]
    amp_tile = (shares / denominator).astype(jnp.bfloat16)

    amps = exchange(jnp.broadcast_to(amp_tile[None], (a_subs, sub_rows, sub_cols)), A_SUM_BITS)
    amps = amps.reshape(pa_width, sub_cols)
    other_amps = lax.ppermute(amps, B_SUM_BITS, swap)

    def contribution(cols, amp_cols):
        return lax.dot_general(cols, amp_cols, (((1,), (1,)), ((), ())), preferred_element_type=jnp.float32)

    own = lax.optimization_barrier(contribution(half_of(b_sub), amps))
    contrib = own + contribution(half_of(1 - b_sub), other_amps)
    returned = exchange(contrib.reshape(peers, rows, pa_width).astype(jnp.bfloat16), AB_BITS)
    returned = pltpu.with_memory_space_constraint(returned, pltpu.VMEM)
    return place_rows(left_list, returned, occ_count, a_parts, b_parts)


def solution(mesh):
    fine = Mesh(np.asarray(mesh.devices).reshape((2,) * len(ALL_BITS)), ALL_BITS)
    placed = (P(None, ALL_BITS, None), P(), P(), P(), P())
    return jax.shard_map(body, mesh=fine, in_specs=placed, out_specs=P(None, ALL_BITS, None), check_vma=False)
```
